128 devices in a mesh: shell: 16 (over z, x), blk: 8 (over y, core).
Axes of the slice: x: 4, y: 4, z: 4, core: 2. Of those that a mesh axis runs over, the one named last changes fastest.
Arguments:
- cycle_fourier: bfloat16 [512, 2, 192, 1024], P('shell', None, None, 'blk'), may hold values from -6 to 6
- legendre: bfloat16 [192, 768, 1024], P('shell', None, 'blk'), may hold values from -0.1875 to 0.1875
- azimuth_orders: int32 [192], replicated, may hold values from 0 to 767, as said below
- multipole: int32 [768], P(('shell', 'blk')), may hold values from 0 to 767, each once
- bessel: bfloat16 [768, 512, 512], P(('shell', 'blk')), may hold values from -0.25 to 0.25
- signal_power: float32 [768, 512], P(('shell', 'blk')), may hold values from 0.1 to 10
- noise_power: float32 [768, 512], P(('shell', 'blk')), may hold values from 0.1 to 10
Outputs:
- filtered: bfloat16 [768, 512, 384], P('shell', 'blk')
The draws below stay inside these ranges and needn't reach their ends.
Inputs may be any that keep to these rules, and one draw needn't show every extreme that they name: `azimuth_orders`: distinct orders; 0 and 767 always among them. Each multipole 0 to 767 appears once.
All inputs are finite; a program needn't handle non-finite values.
Results may differ from the reference program's by a relative error of at most 0.017.
Values may be sent and summed in bfloat16 or wider, within the bound.
A program may use at most 128 MiB of HBM per device.

```python
import math
import jax
import jax.numpy as jnp
from jax import lax

L = 768
CYCLES = 1024
SHELLS = 512
M_COLS = 192
N_BLK = 8


def draw_azimuth_orders(key, part):
    inner = jax.random.permutation(jax.random.fold_in(key, 11), L - 2)[:M_COLS - 2] + 1
    joined = jnp.concatenate([jnp.array([0, L - 1], jnp.int32), inner.astype(jnp.int32)])
    return jax.random.permutation(jax.random.fold_in(key, 12), joined).astype(jnp.int32)


def steps_of(rng, extent, cuts, smallest, top_value):
    factor_of, own = 1.0, jax.random.fold_in(rng, 6)
    for axis_at, shards_of in cuts:
        draws = jnp.exp(jax.random.uniform(jax.random.fold_in(own, axis_at), (shards_of,), jnp.float32, smallest / len(cuts), top_value / len(cuts)))
        factor_of = factor_of * jnp.repeat(draws, extent[axis_at] // shards_of).reshape([-1 if axis == axis_at else 1 for axis in range(len(extent))])
    return factor_of


def noise(own_key, dims, width, reach, shards=(), dtype=jnp.bfloat16):
    result = width * jax.random.normal(own_key, dims, jnp.float32)
    if shards:
        result = result * steps_of(own_key, dims, shards, -0.22, 0.18)
    return jnp.clip(result, -reach, reach).astype(dtype)


def setup_inputs(seed: int = 0) -> dict:
    key_list = jax.random.split(jax.random.key(seed), 8)
    return {
        "cycle_fourier": noise(key_list[0], (SHELLS, 2, M_COLS, CYCLES), 1.0, 6.0, ((0, 16), (3, 8))),
        "legendre": noise(key_list[1], (M_COLS, L, CYCLES), CYCLES ** -0.5, 0.1875, ((0, 16), (2, 8))),
        "azimuth_orders": draw_azimuth_orders(jax.random.fold_in(key_list[7], 71), 0),
        "multipole": jax.random.permutation(key_list[3], L).astype(jnp.int32),
        "bessel": noise(key_list[4], (L, SHELLS, SHELLS), SHELLS ** -0.5, 0.25, ((0, 128),)),
        "signal_power": jnp.clip(jnp.exp(math.log(10.0) - 4.6051702 * jax.random.uniform(key_list[5], (L, SHELLS), jnp.float32) ** steps_of(key_list[5], (L, SHELLS), ((0, 128),), -0.2, 0.2)), 0.1, 10.0),
        "noise_power": jnp.clip(jnp.exp(math.log(10.0) - 4.6051702 * jax.random.uniform(key_list[6], (L, SHELLS), jnp.float32) ** steps_of(key_list[6], (L, SHELLS), ((0, 128),), -0.2, 0.2)), 0.1, 10.0),
    }


def reference(cycle_fourier, legendre, azimuth_orders, multipole, bessel, signal_power, noise_power):
    cycle_span = CYCLES // N_BLK
    accumulated = jnp.zeros((L, M_COLS, 2, SHELLS), jnp.float32)
    for blocks in range(N_BLK):
        fields = cycle_fourier[:, :, :, blocks * cycle_span:(blocks + 1) * cycle_span].astype(jnp.float32)
        tables = legendre[:, :, blocks * cycle_span:(blocks + 1) * cycle_span].astype(jnp.float32)
        partial_value = jnp.einsum("jir,scjr->ijcs", tables, fields).astype(jnp.bfloat16)
        partial_value = lax.optimization_barrier(partial_value)
        accumulated = accumulated + partial_value.astype(jnp.float32)
    allowed = multipole[:, None] >= azimuth_orders[None, :]
    coeffs = jnp.where(allowed[:, :, None, None], accumulated, 0.0).astype(jnp.bfloat16)
    bessel_wide = bessel.astype(jnp.float32)
    forward = jnp.einsum("iks,ijcs->ijck", bessel_wide, coeffs.astype(jnp.float32))
    wiener = signal_power / (signal_power + noise_power)
    scaled = (forward * wiener[:, None, None, :]).astype(jnp.bfloat16)
    filtered = jnp.einsum("iks,ijck->isjc", bessel_wide, scaled.astype(jnp.float32))
    return filtered.reshape(L, SHELLS, 2 * M_COLS).astype(jnp.bfloat16)
```

```python
import jax
import jax.numpy as jnp
from jax import lax
from jax.sharding import Mesh, PartitionSpec as P

PLANE = ("z", "x", "y")
ALL = ("z", "x", "y", "core")
SHELL = ("z", "x")
BLK = ("y", "core")


def body(cycle_fourier, legendre, azimuth_orders, multipole, bessel, signal_power, noise_power):
    shells, _, cols, cycles = cycle_fourier.shape
    ny = lax.axis_size("y")
    per = cols // (lax.axis_size("z") * lax.axis_size("x") * ny)
    planes = cols // per
    f = cycle_fourier.transpose(2, 1, 0, 3)
    f = lax.all_to_all(f, PLANE, split_axis=0, concat_axis=0, tiled=True)
    f = f.reshape(planes // ny, ny, per, 2, shells, cycles)
    rows = legendre.shape[1]
    t = lax.all_to_all(legendre, "y", split_axis=0, concat_axis=0, tiled=True)
    t = t.reshape(ny, per, rows, cycles)
    part = jnp.einsum("yjir,ayjcsr->cjias", t, f, preferred_element_type=jnp.float32)
    part = part.astype(jnp.bfloat16).reshape(2, per, rows, planes // ny * shells)
    both = lax.all_to_all(part, "core", split_axis=0, concat_axis=0, tiled=True)
    c = (both[0].astype(jnp.float32) + both[1].astype(jnp.float32)).astype(jnp.bfloat16)
    total = c.shape[-1]
    devices = planes * 2
    local = rows // devices
    c = c.reshape(per, devices, local, total).transpose(1, 2, 0, 3)
    c = lax.all_to_all(c, ALL, split_axis=0, concat_axis=0, tiled=True)
    c = c.reshape(planes, 2, local, per, total).transpose(2, 0, 3, 1, 4)
    coeffs = c.reshape(local, cols, 2, total)
    allowed = multipole[:, None] >= azimuth_orders[None, :]
    coeffs = jnp.where(allowed[:, :, None, None], coeffs, jnp.zeros((), jnp.bfloat16))
    coeffs = coeffs.reshape(local, cols * 2, total)
    forward = jnp.einsum("iks,ijs->ikj", bessel, coeffs, preferred_element_type=jnp.float32)
    wiener = signal_power / (signal_power + noise_power)
    scaled = (forward * wiener[:, :, None]).astype(jnp.bfloat16)
    out = jnp.einsum("iks,ikj->isj", bessel, scaled, preferred_element_type=jnp.float32)
    return lax.all_to_all(out.astype(jnp.bfloat16), BLK, split_axis=1, concat_axis=0, tiled=True)


def solution(mesh):
    fine = Mesh(mesh.devices.reshape(4, 4, 4, 2), ALL)
    return jax.shard_map(
        body,
        mesh=fine,
        in_specs=(
            P(SHELL, None, None, BLK),
            P(SHELL, None, BLK),
            P(),
            P(ALL),
            P(ALL, None, None),
            P(ALL, None),
            P(ALL, None),
        ),
        out_specs=P(SHELL, BLK, None),
        check_vma=False,
    )
```

```python
import jax
import jax.numpy as jnp
from jax import lax
from jax.experimental import pallas as pl
from jax.experimental.pallas import tpu as pltpu
from jax.sharding import Mesh, PartitionSpec as P

ALL = ("z", "x", "y", "core")
SHELL = ("z", "x")
BLK = ("y", "core")
MESH = pl.DeviceIdType.MESH
BF16, F32 = jnp.bfloat16, jnp.float32
ROWS, CYC, SH = 768, 128, 32
NP, ND, PER = 64, 128, 3


def place():
    return tuple(lax.axis_index(n) for n in ALL)


def remote(src, dst, send, recv, z, x, y, c):
    return pltpu.make_async_remote_copy(
        src_ref=src, dst_ref=dst, send_sem=send, recv_sem=recv,
        device_id=(z, x, y, c), device_id_type=MESH,
    )


def drain(ref, sem):
    pltpu.make_async_copy(ref, ref, sem).wait()


def gather_kernel(f_ref, l_ref, out_ref, fr, lr, ps, pr, cf, cs,
                  f_send, f_recv, l_send, l_recv, p_send, p_recv, c_send, c_recv):
    z, x, y, c = place()
    plane = (z * 4 + x) * 4 + y
    me = plane * 2 + c
    barrier = pltpu.get_barrier_semaphore()

    def greet(d, _):
        pl.semaphore_signal(
            barrier, inc=1, device_id_type=MESH,
            device_id=((z + d // 32) % 4, (x + d // 8) % 4, (y + d // 2) % 4, (c + d) % 2),
        )
        return 0

    lax.fori_loop(1, ND, greet, 0)
    pl.semaphore_wait(barrier, ND - 1)

    for j in range(PER):
        for d in (2, 1, 3):
            ty = (y + d) % 4
            remote(l_ref.at[ty * PER + j], lr.at[j, y], l_send.at[j], l_recv.at[j], z, x, ty, c).start()
        pltpu.make_async_copy(l_ref.at[y * PER + j], lr.at[j, y], l_recv.at[j]).start()

        def send(d, _, j=j):
            tz, tx, ty = (z + d // 16) % 4, (x + d // 4) % 4, (y + d) % 4
            t = (tz * 4 + tx) * 4 + ty
            remote(f_ref.at[t * PER + j], fr.at[j, z * 4 + x, y], f_send.at[j], f_recv.at[j], tz, tx, ty, c).start()
            return 0

        lax.fori_loop(1, NP, send, 0)
        pltpu.make_async_copy(f_ref.at[plane * PER + j], fr.at[j, z * 4 + x, y], f_recv.at[j]).start()

    def half(j, part, m):
        lhs = jnp.concatenate([lr[j, b, pl.ds(m * 128, 128), :] for b in range(4)], axis=1)
        rhs = jnp.concatenate(
            [fr[j, :, b, part].reshape(16 * SH, CYC) for b in range(4)], axis=1
        )
        return lax.dot_general(lhs, rhs, (((1,), (1,)), ((), ())), preferred_element_type=F32)

    def spread(j, part):
        def step(m, _):
            acc = half(j, part, m)
            for q in range(4):
                cf[pl.ds(m * 512 + q, 128, stride=4), :] = acc[:, q * 128:(q + 1) * 128]
            return 0

        lax.fori_loop(0, ROWS // 128, step, 0)

    for j in range(PER):
        drain(lr.at[j], l_recv.at[j])
        drain(fr.at[j], f_recv.at[j])
        spread(j, 1 - c)

        def keep(m, _, j=j):
            rows = pl.ds(m * 512, 512)
            ps[j, rows, :] = cf[rows, :].astype(BF16)
            return 0

        lax.fori_loop(0, ROWS // 128, keep, 0)
        swap = remote(ps.at[j], pr.at[j], p_send.at[j], p_recv.at[j], z, x, y, 1 - c)
        swap.start()
        spread(j, c)
        swap.wait_recv()

        def add(m, _, j=j):
            rows = pl.ds(m * 512, 512)
            cs[j, rows, :] = (cf[rows, :] + pr[j, rows, :].astype(F32)).astype(BF16)
            return 0

        lax.fori_loop(0, ROWS // 128, add, 0)

        def post(d, _, j=j):
            tz, tx, ty, tc = (z + d // 32) % 4, (x + d // 8) % 4, (y + d // 2) % 4, (c + d) % 2
            t = ((tz * 4 + tx) * 4 + ty) * 2 + tc
            remote(cs.at[j, pl.ds(t * 24, 24)], out_ref.at[j, me], c_send.at[j], c_recv.at[j], tz, tx, ty, tc).start()
            return 0

        lax.fori_loop(1, ND, post, 0)
        pltpu.make_async_copy(cs.at[j, pl.ds(me * 24, 24)], out_ref.at[j, me], c_recv.at[j]).start()

    for j in range(PER):
        drain(out_ref.at[j], c_recv.at[j])
        drain(lr.at[j, pl.ds(0, 3)], l_send.at[j])
        drain(f_ref.at[pl.ds(0, NP - 1)], f_send.at[j])
        drain(out_ref.at[j, pl.ds(0, ND - 1)], c_send.at[j])
        remote(ps.at[j], pr.at[j], p_send.at[j], p_recv.at[j], z, x, y, 1 - c).wait_send()


def gather(f, t):
    dma = pltpu.SemaphoreType.DMA
    return pl.pallas_call(
        gather_kernel,
        out_shape=jax.ShapeDtypeStruct((PER, ND, 24, 128), BF16),
        in_specs=[pl.BlockSpec(memory_space=pl.ANY)] * 2,
        out_specs=pl.BlockSpec(memory_space=pl.ANY),
        scratch_shapes=[
            pltpu.VMEM((PER, 16, 4, 2, SH, CYC), BF16),
            pltpu.VMEM((PER, 4, ROWS, CYC), BF16),
            pltpu.VMEM((PER, ROWS * 4, 128), BF16),
            pltpu.VMEM((PER, ROWS * 4, 128), BF16),
            pltpu.VMEM((ROWS * 4, 128), F32),
            pltpu.VMEM((PER, ROWS * 4, 128), BF16),
        ] + [dma((PER,))] * 8,
        compiler_params=pltpu.CompilerParams(collective_id=0, has_side_effects=True, vmem_limit_bytes=40 * 2**20),
        name="gather",
    )(f, t)


def radial_kernel(c_ref, b_ref, s_ref, n_ref, k_ref, out_ref, xf, xi, os, o_send, o_recv):
    z, x, y, c = place()
    blk = y * 2 + c
    barrier = pltpu.get_barrier_semaphore()
    for d in range(1, 8):
        pl.semaphore_signal(
            barrier, inc=1, device_id_type=MESH, device_id=(z, x, (y + d // 2) % 4, (c + d) % 2)
        )

    def widen(m, _):
        for j in range(PER):
            xf[pl.ds((j * 8 + m) * 384, 384), :] = c_ref[j, pl.ds(m * 16, 16)].reshape(384, 128).astype(F32)
        return 0

    lax.fori_loop(0, 8, widen, 0)
    pl.semaphore_wait(barrier, 7)

    def row(i, _):
        for q in range(4):
            for j in range(PER):
                for h in range(2):
                    xi[q, pl.ds(2 * j + h, 64, stride=6), :] = xf[pl.ds(j * 3072 + h * 24 + i * 4 + q, 64, stride=48), :]
        rows = jnp.concatenate([xi[q].astype(BF16) for q in range(4)], axis=1)
        basis = b_ref[i]
        forward = lax.dot_general(rows, basis, (((1,), (1,)), ((), ())), preferred_element_type=F32)
        power = s_ref[pl.ds(i, 1), :]
        scaled = (forward * (power / (power + n_ref[pl.ds(i, 1), :]))).astype(BF16)
        out = lax.dot_general(basis, scaled, (((0,), (1,)), ((), ())), preferred_element_type=F32)
        out = jnp.where(k_ref[pl.ds(i, 1), :] > 0.5, out, 0.0)
        os[i] = out.astype(BF16)
        for d in range(1, 8):
            ty, tc = (y + d // 2) % 4, (c + d) % 2
            remote(os.at[i, pl.ds((ty * 2 + tc) * 64, 64)], out_ref.at[blk * 6 + i], o_send, o_recv, z, x, ty, tc).start()
        pltpu.make_async_copy(os.at[i, pl.ds(blk * 64, 64)], out_ref.at[blk * 6 + i], o_recv).start()
        return 0

    lax.fori_loop(0, 6, row, 0)
    drain(out_ref, o_recv)
    drain(out_ref.at[pl.ds(0, 42)], o_send)


def radial(coeffs, bessel, signal, noise, keep):
    dma = pltpu.SemaphoreType.DMA
    return pl.pallas_call(
        radial_kernel,
        out_shape=jax.ShapeDtypeStruct((48, 64, 384), BF16),
        in_specs=[pl.BlockSpec(memory_space=pltpu.VMEM)] * 5,
        out_specs=pl.BlockSpec(memory_space=pl.ANY),
        scratch_shapes=[
            pltpu.VMEM((PER * ND * 24, 128), F32),
            pltpu.VMEM((4, 384, 128), F32),
            pltpu.VMEM((6, 512, 384), BF16),
            dma, dma,
        ],
        compiler_params=pltpu.CompilerParams(collective_id=1, has_side_effects=True, vmem_limit_bytes=40 * 2**20),
        name="radial",
    )(coeffs, bessel, signal, noise, keep)


def body(cycle_fourier, legendre, azimuth_orders, multipole, bessel, signal_power, noise_power):
    coeffs = gather(cycle_fourier.transpose(2, 1, 0, 3), legendre)
    allowed = multipole[:, None] >= jnp.repeat(azimuth_orders, 2)[None, :]
    return radial(coeffs, bessel, signal_power, noise_power, allowed.astype(F32))


def solution(mesh):
    fine = Mesh(mesh.devices.reshape(4, 4, 4, 2), ALL)
    return jax.shard_map(
        body,
        mesh=fine,
        in_specs=(
            P(SHELL, None, None, BLK),
            P(SHELL, None, BLK),
            P(),
            P(ALL),
            P(ALL, None, None),
            P(ALL, None),
            P(ALL, None),
        ),
        out_specs=P(SHELL, BLK, None),
        check_vma=False,
    )
```

```python
import jax
import jax.numpy as jnp
from jax import lax
from jax.experimental import pallas as pl
from jax.experimental.pallas import tpu as pltpu
from jax.sharding import Mesh, PartitionSpec as P

ALL = ("z", "x", "y", "core")
SHELL = ("z", "x")
BLK = ("y", "core")
MESH = pl.DeviceIdType.MESH
BF16, F32 = jnp.bfloat16, jnp.float32
ROWS, CYC, SH = 768, 128, 32
NP, ND, PER = 64, 128, 3


def place():
    return tuple(lax.axis_index(n) for n in ALL)


def remote(src, dst, send, recv, z, x, y, c):
    return pltpu.make_async_remote_copy(
        src_ref=src, dst_ref=dst, send_sem=send, recv_sem=recv,
        device_id=(z, x, y, c), device_id_type=MESH,
    )


def drain(ref, sem):
    pltpu.make_async_copy(ref, ref, sem).wait()


def kernel(f_ref, l_ref, b_ref, s_ref, n_ref, k_ref, out_ref,
           fin, ff, ft, fr, lr, ps, pr, cf, cs, cr, xf, xi, os, bes,
           in_sem, f_send, f_recv, l_send, l_recv, p_send, p_recv, c_send, c_recv, o_send, o_recv):
    z, x, y, c = place()
    plane = (z * 4 + x) * 4 + y
    me = plane * 2 + c
    blk = y * 2 + c
    load = pltpu.make_async_copy(f_ref, fin, in_sem.at[0])
    load.start()
    barrier = pltpu.get_barrier_semaphore()

    def greet(d, _):
        pl.semaphore_signal(
            barrier, inc=1, device_id_type=MESH,
            device_id=((z + d // 32) % 4, (x + d // 8) % 4, (y + d // 2) % 4, (c + d) % 2),
        )
        return 0

    lax.fori_loop(1, ND, greet, 0)
    basis_load = pltpu.make_async_copy(b_ref, bes, in_sem.at[1])
    basis_load.start()
    load.wait()

    def lift(i, _):
        for h in range(2):
            ff[h, pl.ds(i * 192, 192), :] = fin[i, h].astype(F32)
        return 0

    lax.fori_loop(0, SH, lift, 0)
    pl.semaphore_wait(barrier, ND - 1)

    for j in range(PER):
        for d in (2, 1, 3):
            ty = (y + d) % 4
            remote(l_ref.at[ty * PER + j], lr.at[j, y], l_send.at[j], l_recv.at[j], z, x, ty, c).start()
        pltpu.make_async_copy(l_ref.at[y * PER + j], lr.at[j, y], l_recv.at[j]).start()

        def turn(t, _, j=j):
            for h in range(2):
                ft[j, t, h] = ff[h, pl.ds(t * PER + j, SH, stride=192), :].astype(BF16)
            return 0

        lax.fori_loop(0, NP, turn, 0)

        def send(d, _, j=j):
            tz, tx, ty = (z + d // 16) % 4, (x + d // 4) % 4, (y + d) % 4
            t = (tz * 4 + tx) * 4 + ty
            remote(ft.at[j, t], fr.at[j, z * 4 + x, y], f_send.at[j], f_recv.at[j], tz, tx, ty, c).start()
            return 0

        lax.fori_loop(1, NP, send, 0)
        pltpu.make_async_copy(ft.at[j, plane], fr.at[j, z * 4 + x, y], f_recv.at[j]).start()

    def half(j, part, m):
        lhs = jnp.concatenate([lr[j, b, pl.ds(m * 128, 128), :] for b in range(4)], axis=1)
        rhs = jnp.concatenate([fr[j, :, b, part].reshape(16 * SH, CYC) for b in range(4)], axis=1)
        return lax.dot_general(lhs, rhs, (((1,), (1,)), ((), ())), preferred_element_type=F32)

    def spread(j, part):
        def step(m, _):
            acc = half(j, part, m)
            for q in range(4):
                cf[pl.ds(m * 512 + q, 128, stride=4), :] = acc[:, q * 128:(q + 1) * 128]
            return 0

        lax.fori_loop(0, ROWS // 128, step, 0)

    for j in range(PER):
        drain(lr.at[j], l_recv.at[j])
        drain(fr.at[j], f_recv.at[j])
        spread(j, 1 - c)

        def keep(m, _, j=j):
            rows = pl.ds(m * 512, 512)
            ps[j, rows, :] = cf[rows, :].astype(BF16)
            return 0

        lax.fori_loop(0, ROWS // 128, keep, 0)
        swap = remote(ps.at[j], pr.at[j], p_send.at[j], p_recv.at[j], z, x, y, 1 - c)
        swap.start()
        spread(j, c)
        swap.wait_recv()

        def add(m, _, j=j):
            rows = pl.ds(m * 512, 512)
            cs[j, rows, :] = (cf[rows, :] + pr[j, rows, :].astype(F32)).astype(BF16)
            return 0

        lax.fori_loop(0, ROWS // 128, add, 0)

        def post(d, _, j=j):
            tz, tx, ty, tc = (z + d // 32) % 4, (x + d // 8) % 4, (y + d // 2) % 4, (c + d) % 2
            t = ((tz * 4 + tx) * 4 + ty) * 2 + tc
            remote(cs.at[j, pl.ds(t * 24, 24)], cr.at[j, me], c_send.at[j], c_recv.at[j], tz, tx, ty, tc).start()
            return 0

        lax.fori_loop(1, ND, post, 0)
        pltpu.make_async_copy(cs.at[j, pl.ds(me * 24, 24)], cr.at[j, me], c_recv.at[j]).start()

    basis_load.wait()
    for j in range(PER):
        drain(cr.at[j], c_recv.at[j])

        def widen(m, _, j=j):
            xf[pl.ds((j * 8 + m) * 384, 384), :] = cr[j, pl.ds(m * 16, 16)].reshape(384, 128).astype(F32)
            return 0

        lax.fori_loop(0, 8, widen, 0)

    def row(i, _):
        for q in range(4):
            for j in range(PER):
                for h in range(2):
                    xi[q, pl.ds(2 * j + h, 64, stride=6), :] = xf[pl.ds(j * 3072 + h * 24 + i * 4 + q, 64, stride=48), :]
        rows = jnp.concatenate([xi[q].astype(BF16) for q in range(4)], axis=1)
        basis = bes[i]
        forward = lax.dot_general(rows, basis, (((1,), (1,)), ((), ())), preferred_element_type=F32)
        power = s_ref[pl.ds(i, 1), :]
        scaled = (forward * (power / (power + n_ref[pl.ds(i, 1), :]))).astype(BF16)
        out = lax.dot_general(basis, scaled, (((0,), (1,)), ((), ())), preferred_element_type=F32)
        out = jnp.where(k_ref[pl.ds(i, 1), :] > 0.5, out, 0.0)
        os[i] = out.astype(BF16)
        for d in range(1, 8):
            ty, tc = (y + d // 2) % 4, (c + d) % 2
            remote(os.at[i, pl.ds((ty * 2 + tc) * 64, 64)], out_ref.at[blk * 6 + i], o_send, o_recv, z, x, ty, tc).start()
        pltpu.make_async_copy(os.at[i, pl.ds(blk * 64, 64)], out_ref.at[blk * 6 + i], o_recv).start()
        return 0

    lax.fori_loop(0, 6, row, 0)
    for j in range(PER):
        drain(lr.at[j, pl.ds(0, 3)], l_send.at[j])
        drain(ft.at[j, pl.ds(0, NP - 1)], f_send.at[j])
        drain(cr.at[j, pl.ds(0, ND - 1)], c_send.at[j])
        remote(ps.at[j], pr.at[j], p_send.at[j], p_recv.at[j], z, x, y, 1 - c).wait_send()
    drain(out_ref, o_recv)
    drain(out_ref.at[pl.ds(0, 42)], o_send)


def run(f, t, bessel, signal, noise, keep):
    dma = pltpu.SemaphoreType.DMA
    vmem = pltpu.VMEM
    anywhere = pl.BlockSpec(memory_space=pl.ANY)
    inside = pl.BlockSpec(memory_space=vmem)
    return pl.pallas_call(
        kernel,
        out_shape=jax.ShapeDtypeStruct((48, 64, 384), BF16),
        in_specs=[anywhere] * 3 + [inside] * 3,
        out_specs=anywhere,
        scratch_shapes=[
            vmem((SH, 2, 192, CYC), BF16),
            vmem((2, SH * 192, CYC), F32),
            vmem((PER, NP, 2, SH, CYC), BF16),
            vmem((PER, 16, 4, 2, SH, CYC), BF16),
            vmem((PER, 4, ROWS, CYC), BF16),
            vmem((PER, ROWS * 4, 128), BF16),
            vmem((PER, ROWS * 4, 128), BF16),
            vmem((ROWS * 4, 128), F32),
            vmem((PER, ROWS * 4, 128), BF16),
            vmem((PER, ND, 24, 128), BF16),
            vmem((PER * ND * 24, 128), F32),
            vmem((4, 384, 128), F32),
            vmem((6, 512, 384), BF16),
            vmem((6, 512, 512), BF16),
            dma((2,)),
        ] + [dma((PER,))] * 8 + [dma, dma],
        compiler_params=pltpu.CompilerParams(collective_id=0, has_side_effects=True, vmem_limit_bytes=56 * 2**20),
        name="sphere",
    )(f, t, bessel, signal, noise, keep)


def body(cycle_fourier, legendre, azimuth_orders, multipole, bessel, signal_power, noise_power):
    allowed = multipole[:, None] >= jnp.repeat(azimuth_orders, 2)[None, :]
    return run(cycle_fourier, legendre, bessel, signal_power, noise_power, allowed.astype(F32))


def solution(mesh):
    fine = Mesh(mesh.devices.reshape(4, 4, 4, 2), ALL)
    return jax.shard_map(
        body,
        mesh=fine,
        in_specs=(
            P(SHELL, None, None, BLK),
            P(SHELL, None, BLK),
            P(),
            P(ALL),
            P(ALL, None, None),
            P(ALL, None),
            P(ALL, None),
        ),
        out_specs=P(SHELL, BLK, None),
        check_vma=False,
    )
```

```python
import jax
import jax.numpy as jnp
from jax import lax
from jax.experimental import pallas as pl
from jax.experimental.pallas import tpu as pltpu
from jax.sharding import Mesh, PartitionSpec as P

ALL = ("z", "x", "y", "core")
SHELL = ("z", "x")
BLK = ("y", "core")
MESH = pl.DeviceIdType.MESH
BF16, F32 = jnp.bfloat16, jnp.float32
ROWS, CYC, SH = 768, 128, 32
NP, ND, PER = 64, 128, 3


def place():
    return tuple(lax.axis_index(n) for n in ALL)


def remote(src, dst, send, recv, z, x, y, c):
    return pltpu.make_async_remote_copy(
        src_ref=src, dst_ref=dst, send_sem=send, recv_sem=recv,
        device_id=(z, x, y, c), device_id_type=MESH,
    )


def drain(ref, sem):
    pltpu.make_async_copy(ref, ref, sem).wait()


def kernel(f_ref, l_ref, b_ref, s_ref, n_ref, a_ref, m_ref, out_ref,
           fin, ff, ft, fr, lr, ps, pr, cf, cs, cr, xi, os, bes, az,
           in_sem, f_send, f_recv, l_send, l_recv, p_send, p_recv, c_send, c_recv, o_send, o_recv, plane_in, all_in):
    z, x, y, c = place()
    plane = (z * 4 + x) * 4 + y
    me = plane * 2 + c
    blk = y * 2 + c
    load = pltpu.make_async_copy(f_ref, fin, in_sem.at[0])
    load.start()
    barrier = pltpu.get_barrier_semaphore()

    def tell(sem, dz=0, dx=0, db=0):
        pl.semaphore_signal(
            sem, inc=1, device_id_type=MESH,
            device_id=((z + dz) % 4, (x + dx) % 4, (y + db // 2) % 4, (c + db) % 2),
        )

    for d in range(1, 8):
        tell(barrier, db=d)
    for d in range(1, 4):
        tell(barrier, dx=d)
        tell(barrier, dz=d)
    basis_load = pltpu.make_async_copy(b_ref, bes, in_sem.at[1])
    basis_load.start()
    pl.semaphore_wait(barrier, 13)

    def send_table(j):
        for d in (2, 1, 3):
            ty = (y + d) % 4
            remote(l_ref.at[ty * PER + j], lr.at[j, y], l_send.at[j], l_recv.at[j], z, x, ty, c).start()
        pltpu.make_async_copy(l_ref.at[y * PER + j], lr.at[j, y], l_recv.at[j]).start()

    send_table(0)
    for d in range(1, 4):
        tell(plane_in, dx=d)
    load.wait()

    def lift(i, _):
        for h in range(2):
            ff[pl.ds(h * 6144 + i * 192, 192), :] = fin[i, h].astype(F32)
        return 0

    lax.fori_loop(0, SH // 2, lift, 0)
    pl.semaphore_wait(plane_in, 3)
    for d in range(1, 8):
        tell(all_in, db=d)
    lax.fori_loop(SH // 2, SH, lift, 0)

    for j in range(PER):
        if j > 0:
            send_table(j)

        def turn(t, _, j=j):
            for h in range(2):
                ft[j, t, h] = ff[pl.ds(h * 6144 + t * PER + j, SH, stride=192), :].astype(BF16)
            return 0

        lax.fori_loop(0, NP, turn, 0)
        if j == 0:
            pl.semaphore_wait(all_in, 7)

        def send(d, _, j=j):
            tz, tx, ty = (z + d // 16) % 4, (x + d // 4) % 4, (y + d) % 4
            t = (tz * 4 + tx) * 4 + ty
            remote(ft.at[j, t], fr.at[j, z * 4 + x, y], f_send.at[j], f_recv.at[j], tz, tx, ty, c).start()
            return 0

        lax.fori_loop(1, NP, send, 0)
        pltpu.make_async_copy(ft.at[j, plane], fr.at[j, z * 4 + x, y], f_recv.at[j]).start()

    orders = a_ref[...].reshape(1, 192)
    high = orders // 32
    pick = (lax.broadcasted_iota(jnp.int32, (192, 384), 1) // 2 == lax.broadcasted_iota(jnp.int32, (192, 384), 0)).astype(BF16)
    parts = [
        jnp.dot(jnp.broadcast_to(v.astype(F32), (8, 192)).astype(BF16), pick, preferred_element_type=F32)
        for v in (high, orders - high * 32)
    ]
    az[...] = (parts[0] * 32.0 + parts[1]).astype(jnp.int32)

    def half(j, part, m):
        lhs = jnp.concatenate([lr[j, b, pl.ds(m * 128, 128), :] for b in range(4)], axis=1)
        rhs = jnp.concatenate([fr[j, :, b, part].reshape(16 * SH, CYC) for b in range(4)], axis=1)
        return lax.dot_general(lhs, rhs, (((1,), (1,)), ((), ())), preferred_element_type=F32)

    def spread(j, part):
        def step(m, _):
            acc = half(j, part, m)
            for q in range(4):
                cf[pl.ds(m * 512 + q, 128, stride=4), :] = acc[:, q * 128:(q + 1) * 128]
            return 0

        lax.fori_loop(0, ROWS // 128, step, 0)

    for j in range(PER):
        drain(lr.at[j], l_recv.at[j])
        drain(fr.at[j], f_recv.at[j])
        spread(j, 1 - c)

        def keep(m, _, j=j):
            rows = pl.ds(m * 512, 512)
            ps[j, rows, :] = cf[rows, :].astype(BF16)
            return 0

        lax.fori_loop(0, ROWS // 128, keep, 0)
        swap = remote(ps.at[j], pr.at[j], p_send.at[j], p_recv.at[j], z, x, y, 1 - c)
        swap.start()
        spread(j, c)
        swap.wait_recv()

        def add(m, _, j=j):
            rows = pl.ds(m * 512, 512)
            cs[j, rows, :] = (cf[rows, :] + pr[j, rows, :].astype(F32)).astype(BF16)
            return 0

        lax.fori_loop(0, ROWS // 128, add, 0)

        def post(d, _, j=j):
            tz, tx, ty, tc = (z + d // 32) % 4, (x + d // 8) % 4, (y + d // 2) % 4, (c + d) % 2
            t = ((tz * 4 + tx) * 4 + ty) * 2 + tc
            remote(cs.at[j, pl.ds(t * 24, 24)], cr.at[j, me], c_send.at[j], c_recv.at[j], tz, tx, ty, tc).start()
            return 0

        lax.fori_loop(1, ND, post, 0)
        pltpu.make_async_copy(cs.at[j, pl.ds(me * 24, 24)], cr.at[j, me], c_recv.at[j]).start()

    basis_load.wait()
    for j in range(PER):
        drain(cr.at[j], c_recv.at[j])

        def widen(m, _, j=j):
            ff[pl.ds((j * 8 + m) * 384, 384), :] = cr[j, pl.ds(m * 16, 16)].reshape(384, 128).astype(F32)
            return 0

        lax.fori_loop(0, 8, widen, 0)

    def row(i, _):
        for q in range(4):
            for j in range(PER):
                for h in range(2):
                    xi[q, pl.ds(2 * j + h, 64, stride=6), :] = ff[pl.ds(j * 3072 + h * 24 + i * 4 + q, 64, stride=48), :]
        rows = jnp.concatenate([xi[q].astype(BF16) for q in range(4)], axis=1)
        basis = bes[i]
        forward = lax.dot_general(rows, basis, (((1,), (1,)), ((), ())), preferred_element_type=F32)
        power = s_ref[pl.ds(i, 1), :]
        scaled = (forward * (power / (power + n_ref[pl.ds(i, 1), :]))).astype(BF16)
        out = lax.dot_general(basis, scaled, (((0,), (1,)), ((), ())), preferred_element_type=F32)
        out = jnp.where(az[0:1, :] <= m_ref[i], out, 0.0)
        os[i] = out.astype(BF16)
        for d in range(1, 8):
            ty, tc = (y + d // 2) % 4, (c + d) % 2
            remote(os.at[i, pl.ds((ty * 2 + tc) * 64, 64)], out_ref.at[blk * 6 + i], o_send, o_recv, z, x, ty, tc).start()
        pltpu.make_async_copy(os.at[i, pl.ds(blk * 64, 64)], out_ref.at[blk * 6 + i], o_recv).start()
        return 0

    lax.fori_loop(0, 6, row, 0)
    for j in range(PER):
        drain(lr.at[j, pl.ds(0, 3)], l_send.at[j])
        drain(ft.at[j, pl.ds(0, NP - 1)], f_send.at[j])
        drain(cr.at[j, pl.ds(0, ND - 1)], c_send.at[j])
        remote(ps.at[j], pr.at[j], p_send.at[j], p_recv.at[j], z, x, y, 1 - c).wait_send()
    drain(out_ref, o_recv)
    drain(out_ref.at[pl.ds(0, 42)], o_send)


def run(f, t, bessel, signal, noise, orders, multipole):
    dma = pltpu.SemaphoreType.DMA
    vmem = pltpu.VMEM
    anywhere = pl.BlockSpec(memory_space=pl.ANY)
    inside = pl.BlockSpec(memory_space=vmem)
    return pl.pallas_call(
        kernel,
        out_shape=jax.ShapeDtypeStruct((48, 64, 384), BF16),
        in_specs=[pl.BlockSpec(memory_space=pltpu.HBM)] * 3 + [inside] * 3 + [pl.BlockSpec(memory_space=pltpu.SMEM)],
        out_specs=anywhere,
        scratch_shapes=[
            vmem((SH, 2, 192, CYC), BF16),
            vmem((2 * SH * 192, CYC), F32),
            vmem((PER, NP, 2, SH, CYC), BF16),
            vmem((PER, 16, 4, 2, SH, CYC), BF16),
            vmem((PER, 4, ROWS, CYC), BF16),
            vmem((PER, ROWS * 4, 128), BF16),
            vmem((PER, ROWS * 4, 128), BF16),
            vmem((ROWS * 4, 128), F32),
            vmem((PER, ROWS * 4, 128), BF16),
            vmem((PER, ND, 24, 128), BF16),
            vmem((4, 384, 128), F32),
            vmem((6, 512, 384), BF16),
            vmem((6, 512, 512), BF16),
            vmem((8, 384), jnp.int32),
            dma((2,)),
        ] + [dma((PER,))] * 8 + [dma, dma, pltpu.SemaphoreType.REGULAR, pltpu.SemaphoreType.REGULAR],
        compiler_params=pltpu.CompilerParams(collective_id=0, has_side_effects=True, vmem_limit_bytes=50 * 2**20),
        name="sphere",
    )(f, t, bessel, signal, noise, orders, multipole)


def body(cycle_fourier, legendre, azimuth_orders, multipole, bessel, signal_power, noise_power):
    return run(cycle_fourier, legendre, bessel, signal_power, noise_power, azimuth_orders, multipole)


def solution(mesh):
    fine = Mesh(mesh.devices.reshape(4, 4, 4, 2), ALL)
    return jax.shard_map(
        body,
        mesh=fine,
        in_specs=(
            P(SHELL, None, None, BLK),
            P(SHELL, None, BLK),
            P(),
            P(ALL),
            P(ALL, None, None),
            P(ALL, None),
            P(ALL, None),
        ),
        out_specs=P(SHELL, BLK, None),
        check_vma=False,
    )
```
